32 devices in a mesh: items: 8 (over z, x), frame: 4 (over y, core).
Axes of the slice: x: 2, y: 2, z: 4, core: 2. Of those that a mesh axis runs over, the one named last changes fastest.
Arguments:
- tokens: bfloat16 [6400, 768], P(('items', 'frame')), may hold values from -6 to 6
- visible_place: int32 [32, 200], P(('items', 'frame')), may hold values from 0 to 799, as said below
- item_index: int32 [32, 800], P(('items', 'frame')), may hold values from 0 to 2, as said below
- out_cotangent: bfloat16 [25600, 512], P(('items', 'frame')), may hold values from -6 to 6
- encoder_norm_gain: float32 [768], replicated, may hold values from 0.1 to 1.9
- encoder_norm_shift: float32 [768], replicated, may hold values from -1.75 to 1.75
- encoder_inward: bfloat16 [768, 2304], replicated, may hold values from -0.3125 to 0.3125
- encoder_query_bias: float32 [768], replicated, may hold values from -1.75 to 1.75
- encoder_value_bias: float32 [768], replicated, may hold values from -1.75 to 1.75
- encoder_outward: bfloat16 [768, 768], replicated, may hold values from -0.875 to 0.875
- encoder_outward_bias: float32 [768], replicated, may hold values from -1.75 to 1.75
- encoder_second_gain: float32 [768], replicated, may hold values from 0.1 to 1.9
- encoder_second_shift: float32 [768], replicated, may hold values from -1.75 to 1.75
- encoder_expand: bfloat16 [768, 3072], replicated, may hold values from -0.21875 to 0.21875
- encoder_expand_bias: float32 [3072], replicated, may hold values from -1.75 to 1.75
- encoder_contract: bfloat16 [3072, 768], replicated, may hold values from -0.109375 to 0.109375
- encoder_contract_bias: float32 [768], replicated, may hold values from -1.75 to 1.75
- embed_weight: bfloat16 [768, 512], replicated, may hold values from -0.21875 to 0.21875
- embed_bias: float32 [512], replicated, may hold values from -1.75 to 1.75
- mask_token: float32 [512], replicated, may hold values from -6 to 6
- decoder_norm_gain: float32 [512], replicated, may hold values from 0.1 to 1.9
- decoder_norm_shift: float32 [512], replicated, may hold values from -1.75 to 1.75
- decoder_inward: bfloat16 [512, 1536], replicated, may hold values from -0.375 to 0.375
- decoder_query_bias: float32 [512], replicated, may hold values from -1.75 to 1.75
- decoder_value_bias: float32 [512], replicated, may hold values from -1.75 to 1.75
- decoder_outward: bfloat16 [512, 512], replicated, may hold values from -1 to 1
- decoder_outward_bias: float32 [512], replicated, may hold values from -1.75 to 1.75
- decoder_second_gain: float32 [512], replicated, may hold values from 0.1 to 1.9
- decoder_second_shift: float32 [512], replicated, may hold values from -1.75 to 1.75
- decoder_expand: bfloat16 [512, 2048], replicated, may hold values from -0.25 to 0.25
- decoder_expand_bias: float32 [2048], replicated, may hold values from -1.75 to 1.75
- decoder_contract: bfloat16 [2048, 512], replicated, may hold values from -0.125 to 0.125
- decoder_contract_bias: float32 [512], replicated, may hold values from -1.75 to 1.75
Outputs:
- encoded: bfloat16 [6400, 768], P(('items', 'frame'))
- decoded: bfloat16 [25600, 512], P(('items', 'frame'))
- tokens_grad: float32 [6400, 768], P(('items', 'frame'))
- grad_encoder_norm_gain: float32 [768], P('items')
- grad_encoder_norm_shift: float32 [768], P('items')
- grad_encoder_inward: float32 [768, 2304], P('items', 'frame')
- grad_encoder_query_bias: float32 [768], P('items')
- grad_encoder_value_bias: float32 [768], P('items')
- grad_encoder_outward: float32 [768, 768], P('items', 'frame')
- grad_encoder_outward_bias: float32 [768], P('items')
- grad_encoder_second_gain: float32 [768], P('items')
- grad_encoder_second_shift: float32 [768], P('items')
- grad_encoder_expand: float32 [768, 3072], P('items', 'frame')
- grad_encoder_expand_bias: float32 [3072], P('items')
- grad_encoder_contract: float32 [3072, 768], P('items', 'frame')
- grad_encoder_contract_bias: float32 [768], P('items')
- grad_embed_weight: float32 [768, 512], P('items', 'frame')
- grad_embed_bias: float32 [512], P('items')
- grad_mask_token: float32 [512], P('items')
- grad_decoder_norm_gain: float32 [512], P('items')
- grad_decoder_norm_shift: float32 [512], P('items')
- grad_decoder_inward: float32 [512, 1536], P('items', 'frame')
- grad_decoder_query_bias: float32 [512], P('items')
- grad_decoder_value_bias: float32 [512], P('items')
- grad_decoder_outward: float32 [512, 512], P('items', 'frame')
- grad_decoder_outward_bias: float32 [512], P('items')
- grad_decoder_second_gain: float32 [512], P('items')
- grad_decoder_second_shift: float32 [512], P('items')
- grad_decoder_expand: float32 [512, 2048], P('items', 'frame')
- grad_decoder_expand_bias: float32 [2048], P('items')
- grad_decoder_contract: float32 [2048, 512], P('items', 'frame')
- grad_decoder_contract_bias: float32 [512], P('items')
The draws below stay inside these ranges and needn't reach their ends.
Inputs may be any that keep to these rules, and one draw needn't show every extreme that they name: `visible_place`: each row lists 200 distinct places in increasing order, 0 and 799 always among them. `item_index`: the 4 rows of a group are equal. Item numbers never fall along a row; the 3 items are runs of 400, 200 and 200 places, in an order drawn for each group.
All inputs are finite; a program needn't handle non-finite values.
Results may differ from the reference program's by a relative error of at most 0.028.
Values may be sent and summed in bfloat16 or wider, within the bound.
A program may use at most 192 MiB of HBM per device.

```python
import jax
import jax.numpy as jnp
from jax import lax

E = 768
HEADS_E = 12
EMLP = 3072
DW = 512
HEADS_D = 16
DMLP = 2048
FRAMES = 4
SIDE = 28
TOK_DEV = 200
DEC_DEV = 800
GROUPS = 8
ENC_ROWS = 6400
DEC_ROWS = 25600


def draw_visible_place(key, part):
    row_keys = jax.random.split(key, GROUPS * FRAMES)

    def one_row(row_key):
        inner = jax.random.permutation(row_key, DEC_DEV - 2)[:TOK_DEV - 2].astype(jnp.int32) + 1
        ends = jnp.array([0, DEC_DEV - 1], dtype=jnp.int32)
        return jnp.sort(jnp.concatenate([ends, inner]))
    return jax.vmap(one_row)(row_keys)


def draw_item_index(key, part):
    group_keys = jax.random.split(jax.random.fold_in(key, 17), GROUPS)
    run_sizes = jnp.array([DEC_DEV // 2, DEC_DEV // 4, DEC_DEV // 4], dtype=jnp.int32)
    place_ids = jnp.arange(DEC_DEV, dtype=jnp.int32)

    def one_group(group_key):
        order = jax.random.permutation(group_key, 3).astype(jnp.int32)
        sizes = run_sizes[order]
        first_end = sizes[0]
        second_end = sizes[0] + sizes[1]
        items_row = (place_ids >= first_end).astype(jnp.int32) + (place_ids >= second_end).astype(jnp.int32)
        return jnp.broadcast_to(items_row[None, :], (FRAMES, DEC_DEV))
    return jax.vmap(one_group)(group_keys).reshape(GROUPS * FRAMES, DEC_DEV).astype(jnp.int32)


def with_spikes(result, stream_key, source, target, parts, factor):
    owner, partner = [(jnp.arange(result.shape[position]) // (result.shape[position] // parts)).reshape([-1 if axis == position else 1 for axis in range(result.ndim)]) for position in (source, target)]
    chosen = jax.random.permutation(stream_key, parts)[partner]
    strong = (owner == chosen) | (owner == (partner + parts // 2) % parts)
    return jnp.where(strong, factor * result, result)


def level_of(rng, extent, cuts, least, top_value):
    factor_of, own = 1.0, jax.random.fold_in(rng, 6)
    for dim, shards_of in cuts:
        heights = jnp.exp(jax.random.uniform(jax.random.fold_in(own, dim), (shards_of,), jnp.float32, least / len(cuts), top_value / len(cuts)))
        factor_of = factor_of * jnp.repeat(heights, extent[dim] // shards_of).reshape([-1 if axis == dim else 1 for axis in range(len(extent))])
    return factor_of


def noise(stream_key, shape, deviation, reach, cuts=(), kind=jnp.bfloat16):
    entries = jax.random.normal(stream_key, shape, jnp.float32) * deviation
    if len(cuts) > 0:
        entries = level_of(stream_key, shape, cuts, -0.22, 0.18) * entries
    return jnp.clip(entries, min=-reach, max=reach).astype(kind)


def noise_with(own_key, extent, width, reach, cuts, heavy, kind=jnp.bfloat16):
    values = width * jax.random.normal(own_key, extent, jnp.float32)
    if cuts:
        values = values * level_of(own_key, extent, cuts, -0.22, 0.18)
    return jnp.clip(with_spikes(values, jax.random.fold_in(own_key, 3), *heavy), -reach, reach).astype(kind)


def setup_inputs(seed: int = 0) -> dict:
    seeds = jax.random.split(jax.random.key(seed), 34)
    return {
        "tokens": noise_with(seeds[0], (ENC_ROWS, E), 1.0, 6.0, ((0, 32),), (0, 1, 32, 2.75)),
        "visible_place": draw_visible_place(jax.random.fold_in(seeds[33], 71), 0),
        "item_index": draw_item_index(jax.random.fold_in(seeds[33], 71), 0),
        "out_cotangent": noise_with(seeds[3], (DEC_ROWS, DW), 1.0, 6.0, ((0, 32),), (0, 1, 32, 2.75)),
        "encoder_norm_gain": jnp.clip(1.0 + 0.18 * jax.random.normal(seeds[4], (E,), jnp.float32), 0.1, 1.9),
        "encoder_norm_shift": noise(seeds[5], (E,), 0.3, 1.75, (), jnp.float32),
        "encoder_inward": noise(seeds[6], (E, 3 * E), (E // 2) ** -0.5, 0.3125),
        "encoder_query_bias": noise(seeds[7], (E,), 0.3, 1.75, (), jnp.float32),
        "encoder_value_bias": noise(seeds[8], (E,), 0.3, 1.75, (), jnp.float32),
        "encoder_outward": noise(seeds[9], (E, E), (E // 16) ** -0.5, 0.875),
        "encoder_outward_bias": noise(seeds[10], (E,), 0.3, 1.75, (), jnp.float32),
        "encoder_second_gain": jnp.clip(1.0 + 0.18 * jax.random.normal(seeds[11], (E,), jnp.float32), 0.1, 1.9),
        "encoder_second_shift": noise(seeds[12], (E,), 0.3, 1.75, (), jnp.float32),
        "encoder_expand": noise(seeds[13], (E, EMLP), E ** -0.5, 0.21875),
        "encoder_expand_bias": noise(seeds[14], (EMLP,), 0.3, 1.75, (), jnp.float32),
        "encoder_contract": noise(seeds[15], (EMLP, E), EMLP ** -0.5, 0.109375),
        "encoder_contract_bias": noise(seeds[16], (E,), 0.3, 1.75, (), jnp.float32),
        "embed_weight": noise(seeds[17], (E, DW), E ** -0.5, 0.21875),
        "embed_bias": noise(seeds[18], (DW,), 0.3, 1.75, (), jnp.float32),
        "mask_token": noise(seeds[19], (DW,), 1.0, 6.0, (), jnp.float32),
        "decoder_norm_gain": jnp.clip(1.0 + 0.18 * jax.random.normal(seeds[20], (DW,), jnp.float32), 0.1, 1.9),
        "decoder_norm_shift": noise(seeds[21], (DW,), 0.3, 1.75, (), jnp.float32),
        "decoder_inward": noise(seeds[22], (DW, 3 * DW), (DW // 2) ** -0.5, 0.375),
        "decoder_query_bias": noise(seeds[23], (DW,), 0.3, 1.75, (), jnp.float32),
        "decoder_value_bias": noise(seeds[24], (DW,), 0.3, 1.75, (), jnp.float32),
        "decoder_outward": noise(seeds[25], (DW, DW), (DW // 16) ** -0.5, 1.0),
        "decoder_outward_bias": noise(seeds[26], (DW,), 0.3, 1.75, (), jnp.float32),
        "decoder_second_gain": jnp.clip(1.0 + 0.18 * jax.random.normal(seeds[27], (DW,), jnp.float32), 0.1, 1.9),
        "decoder_second_shift": noise(seeds[28], (DW,), 0.3, 1.75, (), jnp.float32),
        "decoder_expand": noise(seeds[29], (DW, DMLP), DW ** -0.5, 0.25),
        "decoder_expand_bias": noise(seeds[30], (DMLP,), 0.3, 1.75, (), jnp.float32),
        "decoder_contract": noise(seeds[31], (DMLP, DW), DMLP ** -0.5, 0.125),
        "decoder_contract_bias": noise(seeds[32], (DW,), 0.3, 1.75, (), jnp.float32),
    }


EPSILON = 1e-06
NEGATIVE = -1e+30
HIGHEST = lax.Precision.HIGHEST

@jax.custom_vjp
def low(v):
    return lax.optimization_barrier(v.astype(jnp.bfloat16)).astype(jnp.float32)

@jax.custom_vjp
def low_back(v):
    return v

def low_keep(v):
    return (low(v), None)

def low_pass(kept, grad):
    return (grad,)

def back_keep(v):
    return (v, None)

def back_low(kept, grad):
    return (low(grad),)
low.defvjp(low_keep, low_pass)
low_back.defvjp(back_keep, back_low)

def sincos(count, angles_in):
    half_count = count // 2
    frequency = 10000.0 ** (-jnp.arange(half_count, dtype=jnp.float32) / half_count)
    angles = angles_in[:, None] * frequency[None, :]
    return jnp.concatenate([jnp.sin(angles), jnp.cos(angles)], axis=1)

def placement_code(frame_value, places, model_width):
    first_part = model_width // 4
    other_part = (model_width - first_part) // 2
    frame_col = jnp.zeros(places.shape, jnp.float32) + frame_value
    return jnp.concatenate([sincos(first_part, frame_col), sincos(other_part, (places // SIDE).astype(jnp.float32)), sincos(other_part, (places % SIDE).astype(jnp.float32))], axis=1)

def normalize(values_in, gain, shift):
    average = lax.optimization_barrier(jnp.mean(values_in, axis=-1, keepdims=True))
    centred = values_in - average
    spread = lax.optimization_barrier(jnp.mean(centred * centred, axis=-1, keepdims=True))
    return centred * lax.rsqrt(spread + EPSILON) * gain + shift

def attend(queries, keys_all, values_all, same_item, head_count, score_scale):
    row_count, model_width = queries.shape
    head_depth = model_width // head_count

    def split_heads(matrix):
        return matrix.reshape(matrix.shape[0], head_count, head_depth).transpose(1, 0, 2)

    def one_head(pieces):
        query_head, key_head, value_head = pieces
        scores = low_back(jnp.dot(query_head, key_head.T, precision=HIGHEST) * score_scale)
        scores = jnp.where(same_item, scores, NEGATIVE)
        weights = jax.nn.softmax(scores, axis=-1)
        return jnp.dot(low(weights), value_head, precision=HIGHEST)
    outputs = lax.map(jax.checkpoint(one_head), (split_heads(queries), split_heads(keys_all), split_heads(values_all)))
    return outputs.transpose(1, 0, 2).reshape(row_count, model_width)

def residual_block(carried, item_ids, params, head_count):
    norm_gain, norm_shift, inward, query_bias, value_bias, outward, outward_bias, second_gain, second_shift, expand, expand_bias, contract, contract_bias = params
    model_width = carried.shape[1]
    score_scale = (model_width // head_count) ** (-0.5)
    normed = low(normalize(carried, norm_gain, norm_shift))
    all_bias = jnp.concatenate([query_bias, jnp.zeros_like(query_bias), value_bias])
    projected = low(low_back(jnp.dot(normed, inward, precision=HIGHEST) + all_bias))
    queries = projected[:, :model_width]
    keys_all = projected[:, model_width:2 * model_width]
    values_all = projected[:, 2 * model_width:]
    same_item = item_ids[:, None] == item_ids[None, :]
    attended = low(low_back(attend(queries, keys_all, values_all, same_item, head_count, score_scale)))
    mixed_sum = carried + low_back(jnp.dot(attended, outward, precision=HIGHEST) + outward_bias)
    second = low(normalize(mixed_sum, second_gain, second_shift))
    hidden = low_back(jnp.dot(second, expand, precision=HIGHEST) + expand_bias)
    activated = low(jax.nn.gelu(hidden, approximate=False))
    return mixed_sum + low_back(jnp.dot(activated, contract, precision=HIGHEST) + contract_bias)

def group_forward(tokens_group, visible_group, items_group, encoder_params, embed_params, decoder_params):
    frame_ids = jnp.arange(FRAMES, dtype=jnp.int32)
    enc_codes = jax.vmap(lambda frame_id, frame_places: placement_code(frame_id.astype(jnp.float32), frame_places, E))(frame_ids, visible_group)
    carried = tokens_group + enc_codes.reshape(FRAMES * TOK_DEV, E)
    enc_items = jnp.take_along_axis(items_group, visible_group, axis=1).reshape(FRAMES * TOK_DEV)
    encoded = low(residual_block(carried, enc_items, encoder_params, HEADS_E))
    embed_weight, embed_bias, mask_token = embed_params
    embedded = low_back(jnp.dot(encoded, embed_weight, precision=HIGHEST) + embed_bias)
    flat_places = (visible_group + frame_ids[:, None] * DEC_DEV).reshape(FRAMES * TOK_DEV).astype(jnp.int32)
    filled = jnp.broadcast_to(mask_token[None, :], (FRAMES * DEC_DEV, DW)).at[flat_places].set(embedded)
    dec_codes = jax.vmap(lambda frame_id: placement_code(frame_id.astype(jnp.float32), jnp.arange(DEC_DEV, dtype=jnp.int32), DW))(frame_ids)
    filled = filled + dec_codes.reshape(FRAMES * DEC_DEV, DW)
    decoded = residual_block(filled, items_group.reshape(FRAMES * DEC_DEV), decoder_params, HEADS_D)
    return (encoded, decoded)

def reference(tokens, visible_place, item_index, out_cotangent, encoder_norm_gain, encoder_norm_shift, encoder_inward, encoder_query_bias, encoder_value_bias, encoder_outward, encoder_outward_bias, encoder_second_gain, encoder_second_shift, encoder_expand, encoder_expand_bias, encoder_contract, encoder_contract_bias, embed_weight, embed_bias, mask_token, decoder_norm_gain, decoder_norm_shift, decoder_inward, decoder_query_bias, decoder_value_bias, decoder_outward, decoder_outward_bias, decoder_second_gain, decoder_second_shift, decoder_expand, decoder_expand_bias, decoder_contract, decoder_contract_bias):
    initials = (encoder_norm_gain, encoder_norm_shift, encoder_inward, encoder_query_bias, encoder_value_bias, encoder_outward, encoder_outward_bias, encoder_second_gain, encoder_second_shift, encoder_expand, encoder_expand_bias, encoder_contract, encoder_contract_bias, embed_weight, embed_bias, mask_token, decoder_norm_gain, decoder_norm_shift, decoder_inward, decoder_query_bias, decoder_value_bias, decoder_outward, decoder_outward_bias, decoder_second_gain, decoder_second_shift, decoder_expand, decoder_expand_bias, decoder_contract, decoder_contract_bias)
    weights_list = [source.astype(jnp.float32) for source in initials]
    visible_groups = visible_place.reshape(GROUPS, FRAMES, TOK_DEV)
    item_groups = item_index.reshape(GROUPS, FRAMES, DEC_DEV)

    def forward(tokens_float, param_list):
        encoder_params = tuple(param_list[0:13])
        embed_params = tuple(param_list[13:16])
        decoder_params = tuple(param_list[16:29])

        def group_step(carried_zero, group_inputs):
            tokens_group, visible_group, items_group = group_inputs
            encoded, decoded = jax.checkpoint(group_forward)(tokens_group, visible_group, items_group, encoder_params, embed_params, decoder_params)
            return (carried_zero, (encoded, decoded))
        _, (encoded, decoded) = lax.scan(group_step, jnp.zeros((), jnp.float32), (tokens_float.reshape(GROUPS, FRAMES * TOK_DEV, E), visible_groups, item_groups))
        return (encoded.reshape(ENC_ROWS, E), decoded.reshape(DEC_ROWS, DW))
    (encoded, decoded), pullback = jax.vjp(forward, tokens.astype(jnp.float32), weights_list)
    tokens_grad, param_grads = pullback((jnp.zeros_like(encoded), out_cotangent.astype(jnp.float32)))
    return (encoded.astype(jnp.bfloat16), decoded.astype(jnp.bfloat16), tokens_grad, *param_grads)
```

```python
import functools

import numpy as np
import jax
import jax.numpy as jnp
from jax import lax
from jax.experimental import pallas as pl
from jax.experimental.pallas import tpu as pltpu
from jax.sharding import PartitionSpec as P

HEADS_E = 12
HEADS_D = 16
SIDE = 28
EPSILON = 1e-06
MESH = pl.DeviceIdType.MESH

LOG2E = 1.4426950408889634
NEG = -1e30
LANE = 128
def dot_nt(a, b):
    return lax.dot_general(a, b, (((1,), (1,)), ((), ())), preferred_element_type=jnp.float32)
def dot_nn(a, b):
    return lax.dot_general(a, b, (((1,), (0,)), ((), ())), preferred_element_type=jnp.float32)
def head_parts(x, depth):
    per = LANE // depth
    lane = lax.broadcasted_iota(jnp.int32, x.shape, 1) // depth
    return [jnp.where(lane == h, x, jnp.zeros_like(x)) for h in range(per)]

def fwd_kernel(depth, segs, kc, masked, *refs):
    if masked:
        q_ref, k_ref, v_ref, idq_ref, idk_ref, o_ref, lse_ref = refs
    else:
        q_ref, k_ref, v_ref, o_ref, lse_ref = refs
    per = LANE // depth
    coef = depth ** -0.5 * LOG2E
    for g, (q0, qn, k0, kn) in enumerate(segs):
        qm = head_parts(q_ref[q0:q0 + qn, :], depth)
        step = kc if kn % kc == 0 else kn
        def chunk(c, carry):
            ms, ls, accs = carry
            rows = pl.ds(pl.multiple_of(k0 + c * step, 16), step)
            kk = k_ref[rows, :]
            vt = v_ref[rows, :].T
            if masked:
                same = idk_ref[rows, :1] == idq_ref[:1, :qn]
            nm, nl, na = [], [], []
            for h in range(per):
                s = dot_nt(kk, qm[h])
                if masked:
                    s = jnp.where(same, s, NEG)
                m = jnp.maximum(ms[h], jnp.max(s, axis=0, keepdims=True) * coef)
                alpha = jnp.exp2(ms[h] - m)
                p = jnp.exp2(s * coef - m)
                nl.append(ls[h] * alpha + jnp.sum(p, axis=0, keepdims=True))
                na.append(accs[h] * alpha + dot_nn(vt[h * depth:(h + 1) * depth], p.astype(jnp.bfloat16)))
                nm.append(m)
            return nm, nl, na
        init = ([jnp.full((1, qn), NEG * coef, jnp.float32)] * per, [jnp.zeros((1, qn), jnp.float32)] * per, [jnp.zeros((depth, qn), jnp.float32)] * per)
        if kn == step:
            ms, ls, accs = chunk(0, init)
        else:
            ms, ls, accs = lax.fori_loop(0, kn // step, chunk, init)
        out = jnp.concatenate([accs[h] / ls[h] for h in range(per)], axis=0)
        o_ref[q0:q0 + qn, :] = out.T.astype(o_ref.dtype)
        for h in range(per):
            lse_ref[0, g, h:h + 1, :qn] = ms[h] + jnp.log2(ls[h])

def attn_fwd(q, k, v, depth, segs, kc, ids=None):
    rows, n = q.shape; keys = k.shape[0]; tiles = n // LANE
    qpad = max(-(-s[1] // LANE) * LANE for s in segs)
    col = lambda r: pl.BlockSpec((r, LANE), lambda t: (0, t))
    ins = [q, k, v]; specs = [col(rows), col(keys), col(keys)]
    if ids is not None:
        ins += list(ids); specs += [pl.BlockSpec(i.shape, lambda t: (0, 0)) for i in ids]
    per = LANE // depth
    pairs = sum(s[1] * s[3] for s in segs)
    return pl.pallas_call(
        functools.partial(fwd_kernel, depth, segs, kc, ids is not None),
        grid=(tiles,), in_specs=specs,
        out_specs=[col(rows), pl.BlockSpec((1, len(segs), 8, qpad), lambda t: (t, 0, 0, 0))],
        out_shape=[jax.ShapeDtypeStruct((rows, n), jnp.bfloat16), jax.ShapeDtypeStruct((tiles, len(segs), 8, qpad), jnp.float32)],
        compiler_params=pltpu.CompilerParams(vmem_limit_bytes=48 << 20),
        cost_estimate=pl.CostEstimate(flops=4 * pairs * n, bytes_accessed=2 * n * (2 * rows + 2 * keys), transcendentals=pairs * n // depth),
        name="attention_forward",
    )(*ins)

def bwd_kernel(depth, segs, kc, masked, *refs):
    if masked:
        q_ref, k_ref, v_ref, do_ref, o_ref, lse_ref, idq_ref, idk_ref, dq_ref, dk_ref, dv_ref = refs
    else:
        q_ref, k_ref, v_ref, do_ref, o_ref, lse_ref, dq_ref, dk_ref, dv_ref = refs
    per = LANE // depth
    scale = depth ** -0.5
    coef = scale * LOG2E
    pick = (lax.broadcasted_iota(jnp.int32, (8, LANE), 1) // depth == lax.broadcasted_iota(jnp.int32, (8, LANE), 0)).astype(jnp.float32)
    for g, (q0, qn, k0, kn) in enumerate(segs):
        do = do_ref[q0:q0 + qn, :]
        qm = head_parts(q_ref[q0:q0 + qn, :], depth)
        dom = head_parts(do, depth)
        delta = lax.dot_general(pick, do.astype(jnp.float32) * o_ref[q0:q0 + qn, :].astype(jnp.float32), (((1,), (1,)), ((), ())), preferred_element_type=jnp.float32, precision=lax.Precision.HIGHEST)
        step = kc if kn % kc == 0 else kn
        def chunk(c, carry):
            rows = pl.ds(pl.multiple_of(k0 + c * step, 16), step)
            kk = k_ref[rows, :]
            vv = v_ref[rows, :]
            kt = kk.T
            if masked:
                same = idk_ref[rows, :1] == idq_ref[:1, :qn]
            dv = jnp.zeros((step, LANE), jnp.float32)
            dk = jnp.zeros((step, LANE), jnp.float32)
            new = []
            for h in range(per):
                s = dot_nt(kk, qm[h])
                if masked:
                    s = jnp.where(same, s, NEG)
                p = jnp.exp2(s * coef - lse_ref[0, g, h:h + 1, :qn])
                dp = dot_nt(vv, dom[h])
                dv = dv + dot_nn(p.astype(jnp.bfloat16), dom[h])
                ds = (p * (dp - delta[h:h + 1, :])).astype(jnp.bfloat16)
                dk = dk + dot_nn(ds, qm[h])
                new.append(carry[h] + dot_nn(kt[h * depth:(h + 1) * depth], ds))
            dk_ref[rows, :] = (dk * scale).astype(dk_ref.dtype)
            dv_ref[rows, :] = dv.astype(dv_ref.dtype)
            return new
        init = [jnp.zeros((depth, qn), jnp.float32)] * per
        if kn == step:
            dqs = chunk(0, init)
        else:
            dqs = lax.fori_loop(0, kn // step, chunk, init)
        dq_ref[q0:q0 + qn, :] = (jnp.concatenate(dqs, axis=0).T * scale).astype(dq_ref.dtype)

def attn_bwd(q, k, v, do, o, lse, depth, segs, kc, ids=None):
    rows, n = q.shape; keys = k.shape[0]; tiles = n // LANE
    col = lambda r: pl.BlockSpec((r, LANE), lambda t: (0, t))
    ins = [q, k, v, do, o, lse]
    specs = [col(rows), col(keys), col(keys), col(rows), col(rows), pl.BlockSpec((1,) + lse.shape[1:], lambda t: (t, 0, 0, 0))]
    if ids is not None:
        ins += list(ids); specs += [pl.BlockSpec(i.shape, lambda t: (0, 0)) for i in ids]
    pairs = sum(s[1] * s[3] for s in segs)
    return pl.pallas_call(
        functools.partial(bwd_kernel, depth, segs, kc, ids is not None),
        grid=(tiles,), in_specs=specs,
        out_specs=[col(rows), col(keys), col(keys)],
        out_shape=[jax.ShapeDtypeStruct((rows, n), jnp.bfloat16), jax.ShapeDtypeStruct((keys, n), jnp.bfloat16), jax.ShapeDtypeStruct((keys, n), jnp.bfloat16)],
        compiler_params=pltpu.CompilerParams(vmem_limit_bytes=48 << 20),
        cost_estimate=pl.CostEstimate(flops=10 * pairs * n, bytes_accessed=2 * n * (4 * rows + 4 * keys), transcendentals=pairs * n // depth),
        name="attention_backward",
    )(*ins)


def bits_of(count):
    return count.bit_length() - 1


class Plan:
    def __init__(self, n_items, n_frame):
        self.n_items, self.n_frame = n_items, n_frame
        self.digits = [("frame", 1 << b) for b in reversed(range(bits_of(n_frame)))]
        self.digits += [("items", 1 << b) for b in reversed(range(bits_of(n_items)))]

    def mine(self, d):
        axis, weight = self.digits[d]
        return lax.rem(lax.div(lax.axis_index(axis), weight), 2)

    def partner(self, d):
        axis, weight = self.digits[d]
        item, frame = lax.axis_index("items"), lax.axis_index("frame")
        step = weight * (1 - 2 * self.mine(d))
        return (item + step, frame) if axis == "items" else (item, frame + step)


def wgrad_kernel(plan, units, n_vec, *refs):
    nu = len(units)
    nd = len(plan.digits)
    core = bits_of(plan.n_frame) - 1
    pos = 0
    a_refs, b_refs = refs[0:2 * nu:2], refs[1:2 * nu:2]
    pos = 2 * nu
    if n_vec:
        vec_ref = refs[pos]
        pos += 1
    out_refs = refs[pos:pos + nu]
    pos += nu
    if n_vec:
        vec_out = refs[pos]
        pos += 1
    send0, acc0 = refs[pos:pos + nu], refs[pos + nu:pos + 2 * nu]
    pos += 2 * nu
    recv = [refs[pos + u * nd:pos + (u + 1) * nd] for u in range(nu)]
    pos += nu * nd
    if n_vec:
        vsum, vrecv = refs[pos], refs[pos + 1]
        pos += 2
    send_sem, recv_sem = refs[pos], refs[pos + 1]

    barrier = pltpu.get_barrier_semaphore()
    for d in range(nd):
        pl.semaphore_signal(barrier, inc=1, device_id=plan.partner(d), device_id_type=MESH)

    half = plan.n_frame // 2

    def blocks(u, mine, dst):
        transposed = units[u]["t"]

        def one(c, carry):
            f = 2 * c + mine
            if transposed:
                g = dot_nn(b_refs[u][f].T, a_refs[u][...])
            else:
                g = lax.dot_general(a_refs[u][...], b_refs[u][f], (((0,), (0,)), ((), ())), preferred_element_type=jnp.float32)
            size = g.shape[1 if transposed else 0] // plan.n_items
            for i in range(plan.n_items):
                part = g[:, i * size:(i + 1) * size] if transposed else g[i * size:(i + 1) * size]
                index = tuple((i >> b) & 1 for b in reversed(range(bits_of(plan.n_items))))
                dst[(c,) + index] = part.astype(jnp.bfloat16)
            return carry

        lax.fori_loop(0, half, one, 0)

    copies = []

    def send(u, step, src, dst, digit):
        copy = pltpu.make_async_remote_copy(
            src_ref=src, dst_ref=dst, send_sem=send_sem.at[u, step], recv_sem=recv_sem.at[u, step],
            device_id=plan.partner(digit), device_id_type=MESH)
        copy.start()
        copies.append(copy)
        return copy

    orders = [[core] + list(unit["order"]) for unit in units]
    flight = {}
    state = {}

    def view(ref, u, taken, digit, bit):
        left = [d for d in range(nd) if d not in taken]
        at = left.index(digit)
        return ref.at[tuple([slice(None)] * at + [bit])]

    def finish(u, step):
        flight[u, step].wait_recv()
        got = recv[u][step]
        if step == 0:
            got[...] = got[...] + acc0[u][...]
        else:
            taken = orders[u][:step]
            digit = orders[u][step]
            prev = recv[u][step - 1]
            own = view(prev, u, taken, digit, plan.mine(digit))
            got[...] = got[...] + own[...]

    def begin(u, step):
        taken = orders[u][:step]
        digit = orders[u][step]
        prev = recv[u][step - 1]
        src = view(prev, u, taken, digit, 1 - plan.mine(digit))
        flight[u, step] = send(u, step, src, recv[u][step], digit)

    def vstart(step):
        flight["v", step] = send(nu, step, vsum.at[step], vrecv.at[step], step)

    def vfinish(step):
        flight["v", step].wait_recv()
        vsum[step + 1] = vsum[step] + vrecv[step]

    me = plan.mine(core)
    for u in range(nu):
        s0 = send0[u]
        blocks(u, 1 - me, s0)
        if u == 0:
            pl.semaphore_wait(barrier, nd)
            if n_vec:
                vsum[0] = vec_ref[...]
                vstart(0)
        flight[u, 0] = send(u, 0, s0, recv[u][0], core)
        blocks(u, me, acc0[u])
        if u > 0:
            finish(u - 1, 0)
            begin(u - 1, 1)
    finish(nu - 1, 0)
    begin(nu - 1, 1)
    if n_vec:
        vfinish(0)
        vstart(1)
    for step in range(1, nd):
        for u in range(nu):
            finish(u, step)
            if step + 1 < nd:
                begin(u, step + 1)
            else:
                out_refs[u][...] = recv[u][step][...].astype(jnp.float32)
        if n_vec:
            vfinish(step)
            if step + 1 < nd:
                vstart(step + 1)
    if n_vec:
        vec_out[...] = vsum[nd]
    for copy in copies:
        copy.wait_send()


def wgrad_rs(plan, units, vec, cid, name):
    nd = len(plan.digits)
    core = bits_of(plan.n_frame) - 1
    ins, outs, bufs0, recvs = [], [], [], []
    flops = 0
    for unit in units:
        rows, height = unit["a"].shape
        width = unit["b"].shape[2]
        ins += [unit["a"], unit["b"]]
        flops += 2 * rows * height * width * plan.n_frame
        block = (width, height // plan.n_items) if unit["t"] else (height // plan.n_items, width)
        outs.append(jax.ShapeDtypeStruct(block, jnp.float32))
        bufs0.append(pltpu.VMEM((2,) * (nd - 1) + block, jnp.bfloat16))
        recvs += [pltpu.VMEM((2,) * (nd - 1 - s) + block, jnp.bfloat16) for s in range(nd)]
    scratch = bufs0 + bufs0 + recvs
    if vec is not None:
        ins.append(vec)
        outs.append(jax.ShapeDtypeStruct(vec.shape, jnp.float32))
        scratch += [pltpu.VMEM((nd + 1,) + vec.shape, jnp.float32), pltpu.VMEM((nd,) + vec.shape, jnp.float32)]
    count = len(units) + (vec is not None)
    scratch += [pltpu.SemaphoreType.DMA((count, nd))] * 2
    whole = pl.BlockSpec(memory_space=pltpu.VMEM)
    return pl.pallas_call(
        functools.partial(wgrad_kernel, plan, units_static(units), vec is not None),
        out_shape=outs, in_specs=[whole] * len(ins), out_specs=[whole] * len(outs),
        scratch_shapes=scratch,
        compiler_params=pltpu.CompilerParams(collective_id=cid, has_side_effects=True, vmem_limit_bytes=60 << 20),
        cost_estimate=pl.CostEstimate(flops=flops, bytes_accessed=40 << 20, transcendentals=0),
        name=name,
    )(*ins)


def units_static(units):
    return [{"t": unit["t"], "order": unit["order"]} for unit in units]


def code_table(width):
    first = width // 4
    other = (width - first) // 2

    def table(count, positions):
        half_count = count // 2
        frequency = 10000.0 ** (-np.arange(half_count, dtype=np.float64) / half_count)
        angles = np.arange(positions)[:, None] * frequency[None, :]
        return np.concatenate([np.sin(angles), np.cos(angles)], axis=1)

    out = np.zeros((128, width), np.float32)
    out[0:4, :first] = table(first, 4)
    out[32:64, first:first + other] = table(other, 32)
    out[64:64 + SIDE, first + other:] = table(other, SIDE)
    return out


def placement_code(frames, places, width):
    column = lax.broadcasted_iota(jnp.int32, (places.shape[0], 128), 1)
    hot = (column == frames[:, None]) | (column == 32 + (places // SIDE)[:, None]) | (column == 64 + (places % SIDE)[:, None])
    return jnp.dot(hot.astype(jnp.float32), jnp.asarray(code_table(width)), precision=lax.Precision.HIGHEST)


def norm_parts(x):
    centred = x - jnp.mean(x, axis=-1, keepdims=True)
    rstd = lax.rsqrt(jnp.mean(centred * centred, axis=-1, keepdims=True) + EPSILON)
    return centred * rstd, rstd


def norm_back(dn, hat, rstd, gain):
    g = dn * gain
    dx = rstd * (g - jnp.mean(g, axis=-1, keepdims=True) - hat * jnp.mean(g * hat, axis=-1, keepdims=True))
    return dx, jnp.sum(dn * hat, axis=0), jnp.sum(dn, axis=0)


def mm(a, b):
    return jnp.dot(a, b, preferred_element_type=jnp.float32)


def mm_t(a, b):
    return lax.dot_general(a, b, (((1,), (1,)), ((), ())), preferred_element_type=jnp.float32)


def total(x):
    return jnp.sum(x.astype(jnp.float32), axis=0)


def low(x):
    return x.astype(jnp.bfloat16)


def gelu_pair(hidden):
    cdf = 0.5 * (1.0 + lax.erf(hidden * np.float32(0.5 ** 0.5)))
    pdf = jnp.exp(-0.5 * hidden * hidden) * np.float32((2 * np.pi) ** -0.5)
    return hidden * cdf, cdf + hidden * pdf


def post_forward(carried, attended, params):
    (_, _, _, _, _, outward, outward_bias, second_gain, second_shift, expand, expand_bias, contract, contract_bias) = params
    mixed = carried + mm(attended, outward) + outward_bias
    hat, rstd = norm_parts(mixed)
    second = low(hat * second_gain + second_shift)
    hidden = mm(second, expand) + expand_bias
    act, slope = gelu_pair(hidden)
    activated = low(act)
    output = mixed + mm(activated, contract) + contract_bias
    return output, (hat, rstd, second, activated, slope)


def post_backward(gy, kept, params):
    (_, _, _, _, _, outward, _, second_gain, _, expand, _, contract, _) = params
    hat, rstd, second, activated, slope = kept
    dz = low(gy)
    du = low(mm_t(dz, contract) * slope)
    db = mm_t(du, expand)
    part, g_gain, g_shift = norm_back(db, hat, rstd, second_gain)
    dh = gy + part
    da = low(dh)
    do = low(mm_t(da, outward))
    vectors = dict(contract_bias=total(dz), expand_bias=total(du), outward_bias=total(da), second_gain=g_gain, second_shift=g_shift)
    return dh, da, do, du, dz, vectors


def by_frame(x, n_frame):
    rows, width = x.shape
    return x.reshape(rows, n_frame, width // n_frame).transpose(1, 0, 2)


NAMES = ("norm_gain", "norm_shift", "inward", "query_bias", "value_bias", "outward", "outward_bias", "second_gain", "second_shift", "expand", "expand_bias", "contract", "contract_bias")
MATRICES = ("inward", "outward", "expand", "contract")


def body(n_items, n_frame, tokens, visible_place, item_index, out_cotangent, *weights):
    enc_params, (embed_weight, embed_bias, mask_token), dec_params = weights[0:13], weights[13:16], weights[16:29]
    frame = lax.axis_index("frame")
    items_row = item_index[0]
    count, width = items_row.shape[0], mask_token.shape[0]
    vis, wide = tokens.shape
    depth_e, depth_d = wide // HEADS_E, width // HEADS_D
    long, short = count // 2, count // 4
    first_long = items_row[0] == items_row[long - 1]
    last_long = items_row[long] == items_row[count - 1]
    b0 = jnp.where(first_long, 0, jnp.where(last_long, long, short))
    b1 = jnp.where(first_long, long, 0)
    b2 = jnp.where(last_long, short, long + short)
    starts, sizes = (b0, b1, b2), (long, short, short)
    firsts = (0, long, long + short)

    def to_runs(x):
        return jnp.concatenate([lax.dynamic_slice_in_dim(x, s, n, 0) for s, n in zip(starts, sizes)], axis=0)

    def from_runs(x):
        out = jnp.zeros_like(x)
        for s, n, at in zip(starts, sizes, firsts):
            out = lax.dynamic_update_slice_in_dim(out, x[at:at + n], s, 0)
        return out

    end1, end2 = jnp.sum(items_row < 1), jnp.sum(items_row < 2)
    tokens_all = lax.all_gather(tokens, "frame", axis=0, tiled=True)
    places_all = lax.all_gather(visible_place, "frame", axis=0, tiled=True)
    flat = places_all.reshape(-1)
    ids_all = (flat >= end1).astype(jnp.int32) + (flat >= end2).astype(jnp.int32)
    ids_loc = lax.dynamic_slice_in_dim(ids_all, frame * vis, vis)
    frames_e = jnp.repeat(jnp.arange(n_frame, dtype=jnp.int32), vis)
    x0_all = tokens_all.astype(jnp.float32) + placement_code(frames_e, flat, wide)
    ehat_all, erstd_all = norm_parts(x0_all)
    (gain, shift, inward, qb, vb) = enc_params[:5]
    enormed_all = low(ehat_all * gain + shift)
    mine = lambda x: lax.dynamic_slice_in_dim(x, frame * vis, vis, 0)
    enormed = mine(enormed_all)
    ehat, erstd, x0 = mine(ehat_all), mine(erstd_all), mine(x0_all)
    eq = low(mm(enormed, inward[:, :wide]) + qb)
    ek = low(mm(enormed_all, inward[:, wide:2 * wide]))
    ev = low(mm(enormed_all, inward[:, 2 * wide:]) + vb)
    esegs = ((0, vis, 0, n_frame * vis),)
    qpad = -(-vis // LANE) * LANE
    eids = (jnp.broadcast_to(jnp.pad(ids_loc, (0, qpad - vis))[None, :], (8, qpad)), jnp.broadcast_to(ids_all[:, None], (n_frame * vis, LANE)))
    eo, else_ = attn_fwd(eq, ek, ev, depth_e, esegs, 1600, eids)
    enc_out, ekept = post_forward(x0, eo, enc_params)
    encoded = low(enc_out)

    encoded_all = lax.all_gather(encoded, "frame", axis=0, tiled=True)
    delta = mm(encoded_all, embed_weight) + embed_bias - mask_token
    high = low(delta)
    rest = low(delta - high.astype(jnp.float32))
    pair = jnp.concatenate([high.reshape(n_frame, vis, width), rest.reshape(n_frame, vis, width)], axis=1)
    local = jnp.arange(count, dtype=jnp.int32)
    place_runs = jnp.concatenate([s + jnp.arange(n, dtype=jnp.int32) for s, n in zip(starts, sizes)])
    table = jnp.asarray(code_table(width))[:n_frame]
    code = placement_code(jnp.full((count,), 127, jnp.int32), place_runs, width)
    hots, xs, masked = [], [], []
    for at, n in zip(firsts, sizes):
        hot = place_runs[at:at + n][None, :, None] == places_all[:, None, :]
        hots.append(low(hot))
        masked.append(1.0 - jnp.sum(hot.astype(jnp.float32), axis=2))
        picked = jnp.einsum("fpj,fjd->fpd", jnp.concatenate([hots[-1], hots[-1]], axis=2), pair, preferred_element_type=jnp.float32)
        xs.append((picked + mask_token + code[at:at + n][None] + table[:, None, :]).reshape(n_frame * n, width))
    xd_all = jnp.concatenate(xs, axis=0)
    masked_all = jnp.concatenate([m.reshape(-1) for m in masked])
    key_firsts = tuple(n_frame * at for at in firsts)

    def own(x):
        return jnp.concatenate([lax.dynamic_slice_in_dim(x, k + frame * n, n, 0) for k, n in zip(key_firsts, sizes)], axis=0)

    dhat_all, drstd_all = norm_parts(xd_all)
    (gain, shift, inward, qb, vb) = dec_params[:5]
    dnormed_all = low(dhat_all * gain + shift)
    dnormed, dhat, drstd, xd = own(dnormed_all), own(dhat_all), own(drstd_all), own(xd_all)
    dq_in = low(mm(dnormed, inward[:, :width]) + qb)
    dk_in = low(mm(dnormed_all, inward[:, width:2 * width]))
    dv_in = low(mm(dnormed_all, inward[:, 2 * width:]) + vb)
    dsegs = tuple((at, n, k, n_frame * n) for at, n, k in zip(firsts, sizes, key_firsts))
    do_out, dlse = attn_fwd(dq_in, dk_in, dv_in, depth_d, dsegs, 1600)
    dec_out, dkept = post_forward(xd, do_out, dec_params)
    decoded = from_runs(low(dec_out))

    gy = to_runs(out_cotangent).astype(jnp.float32)
    dh, da, do, du, dz, dvec = post_backward(gy, dkept, dec_params)
    gq, gk, gv = attn_bwd(dq_in, dk_in, dv_in, do, do_out, dlse, depth_d, dsegs, 1600)
    gkv = jnp.concatenate([gk, gv], axis=1)
    dn_q = mm_t(gq, inward[:, :width])
    dn_kv = mm_t(gkv, inward[:, width:])
    dx_q, g1, s1 = norm_back(dn_q, dhat, drstd, gain)
    dx_all, g2, s2 = norm_back(dn_kv, dhat_all, drstd_all, gain)
    dvec.update(norm_gain=g1 + g2, norm_shift=s1 + s2, query_bias=total(gq), value_bias=total(gv))
    dx_loc = dh + dx_q
    mask_grad = jnp.sum(dx_all * masked_all[:, None], axis=0) + jnp.sum(dx_loc * own(masked_all)[:, None], axis=0)
    low_all, low_loc = low(dx_all), low(dx_loc)
    de_part = 0.0
    de_loc = 0.0
    for hot, k, at, n in zip(hots, key_firsts, firsts, sizes):
        de_part = de_part + jnp.einsum("fpj,fpd->fjd", hot, low_all[k:k + n_frame * n].reshape(n_frame, n, width), preferred_element_type=jnp.float32)
        de_loc = de_loc + jnp.einsum("pj,pd->jd", lax.dynamic_index_in_dim(hot, frame, 0, keepdims=False), low_loc[at:at + n], preferred_element_type=jnp.float32)
    de_sum = lax.psum_scatter(low(de_part.reshape(n_frame * vis, width)), "frame", scatter_dimension=0, tiled=True)
    de = low(de_sum.astype(jnp.float32) + de_loc)
    own_rows = lax.broadcasted_iota(jnp.int32, (n_frame * count, 1), 0)
    zq = jnp.zeros((n_frame * count, width), jnp.bfloat16)
    for k, at, n in zip(key_firsts, firsts, sizes):
        zq = lax.dynamic_update_slice_in_dim(zq, gq[at:at + n], k + frame * n, 0)
    dproj_d = jnp.concatenate([zq, gkv], axis=1)

    dy = mm_t(de, embed_weight)
    eh, ea, eo_grad, eu, ez, evec = post_backward(dy, ekept, enc_params)
    hq, hk, hv = attn_bwd(eq, ek, ev, eo_grad, eo, else_, depth_e, esegs, 1600, eids)
    hkv = jnp.concatenate([hk, hv], axis=1)
    (gain, shift, inward, qb, vb) = enc_params[:5]
    en_q = mm_t(hq, inward[:, :wide])
    en_kv = mm_t(hkv, inward[:, wide:])
    ex_q, g1, s1 = norm_back(en_q, ehat, erstd, gain)
    ex_all, g2, s2 = norm_back(en_kv, ehat_all, erstd_all, gain)
    evec.update(norm_gain=g1 + g2, norm_shift=s1 + s2, query_bias=total(hq), value_bias=total(hv))
    ex_sum = lax.psum_scatter(low(ex_all), "frame", scatter_dimension=0, tiled=True)
    tokens_grad = eh + ex_q + ex_sum.astype(jnp.float32)
    zq = lax.dynamic_update_slice_in_dim(jnp.zeros((n_frame * vis, wide), jnp.bfloat16), hq, frame * vis, 0)
    dproj_e = jnp.concatenate([zq, hkv], axis=1)

    pairs = {
        ("e", "inward"): (enormed_all, dproj_e), ("e", "outward"): (eo, ea), ("e", "expand"): (ekept[2], eu), ("e", "contract"): (ekept[3], ez),
        ("m", "weight"): (encoded, de),
        ("d", "inward"): (dnormed_all, dproj_d), ("d", "outward"): (do_out, da), ("d", "expand"): (dkept[2], du), ("d", "contract"): (dkept[3], dz),
    }
    vectors = [evec[n] for n in NAMES if n not in MATRICES] + [total(de), mask_grad] + [dvec[n] for n in NAMES if n not in MATRICES]
    packed = jnp.concatenate([v.reshape(n_items, -1) for v in vectors], axis=1)
    tiles = all((a.shape[1] // n_items) % 16 == 0 for a, _ in pairs.values()) and n_frame == 4
    if tiles:
        plan = Plan(n_items, n_frame)
        y, x, z1 = 0, len(plan.digits) - 1, len(plan.digits) - 2
        upper = list(range(2, len(plan.digits) - 2))[::-1]
        orders = [[y, x, z1] + upper, [x, z1, y] + upper, [z1, y, x] + upper]
        unit = lambda key, order, t=False: dict(a=pairs[key][0], b=by_frame(pairs[key][1], n_frame), t=t, order=orders[order])
        keys_d = [("d", "contract"), ("d", "expand"), ("d", "outward"), ("m", "weight"), ("d", "inward")]
        got_d = wgrad_rs(plan, [unit(k, o) for k, o in zip(keys_d, (0, 1, 2, 0, 2))], None, 0, "decoder_weight_gradients")
        keys_e = [("e", "contract"), ("e", "expand"), ("e", "outward"), ("e", "inward")]
        turn = (pairs[keys_e[0]][0].shape[1] // n_items) % LANE == 0
        got_e = wgrad_rs(plan, [unit(k, o, t) for k, o, t in zip(keys_e, (0, 1, 2, 2), (turn, False, False, False))], packed, 1, "encoder_weight_gradients")
        grads = dict(zip(keys_d + keys_e, list(got_d) + list(got_e)))
        if turn:
            grads[keys_e[0]] = grads[keys_e[0]].T
        summed = got_e[-1]
    else:
        grads = {}
        for key, (a, b) in pairs.items():
            part = low(lax.dot_general(a, b, (((0,), (0,)), ((), ())), preferred_element_type=jnp.float32))
            part = lax.psum_scatter(part, "frame", scatter_dimension=1, tiled=True)
            grads[key] = lax.psum_scatter(part, "items", scatter_dimension=0, tiled=True).astype(jnp.float32)
        summed = lax.psum(packed, ("items", "frame"))
    row = lax.dynamic_index_in_dim(summed, lax.axis_index("items"), 0, keepdims=False)
    pieces, at = [], 0
    for v in vectors:
        n = v.shape[0] // n_items
        pieces.append(row[at:at + n])
        at += n
    pieces = iter(pieces)
    enc_grads = [grads["e", n] if n in MATRICES else next(pieces) for n in NAMES]
    mid_grads = [grads["m", "weight"], next(pieces), next(pieces)]
    dec_grads = [grads["d", n] if n in MATRICES else next(pieces) for n in NAMES]
    return (encoded, decoded, tokens_grad, *enc_grads, *mid_grads, *dec_grads)


def solution(mesh):
    rows = P(("items", "frame"), None)
    block = [P("items", "frame") if n in MATRICES else P("items") for n in NAMES]
    return jax.shard_map(
        functools.partial(body, mesh.shape["items"], mesh.shape["frame"]),
        mesh=mesh,
        in_specs=(rows,) * 4 + (P(),) * 29,
        out_specs=(rows,) * 3 + tuple(block) + (P("items", "frame"), P("items"), P("items")) + tuple(block),
        check_vma=False,
    )
```
